512 devices in a mesh: dp: 128 (over y, z, core), feat: 4 (over x).
Axes of the slice: x: 4, y: 8, z: 8, core: 2. Of those that a mesh axis runs over, the one named last changes fastest.
Arguments:
- activations: bfloat16 [131072, 8192], P('dp', 'feat'), may hold values from -6 to 6
- cand_index: int32 [131072], P('dp'), may hold values from 0 to 127
- labels: int32 [8192], P('dp'), may hold values 0 or 1
- counts: int32 [128], P('dp'), may hold values from 1 to 64, as said below
Outputs:
- scores: float32 [131072, 128], P('dp', 'feat')
The draws below stay inside these ranges and needn't reach their ends.
Inputs may be any that keep to these rules, and one draw needn't show every extreme that they name: `counts`: the fullest slab has all 64 prompt slots live.
All inputs are finite; a program needn't handle non-finite values. No bound on the sum of `labels` on one device may be relied on, other than what follows from the above.
Results may differ from the reference program's by a relative error of at most 0.0047.
Values may be sent and summed in bfloat16 or wider, within the bound.
A program may use at most 64 MiB of HBM per device.

```python
import jax
import jax.numpy as jnp
from jax import lax

D = 8192
PER_PROMPT = 16
ROW_DEV = 1024
PROMPT_DEV = 64
SLABS = 128
CANDS = 128
ROWS = 131072
PROMPTS = 8192


def draw_counts(key, part):
    lowest = max(1, PROMPT_DEV // 4)
    values = jax.random.randint(key, (SLABS,), lowest, PROMPT_DEV + 1)
    chosen_slab = jax.random.randint(jax.random.fold_in(key, 7), (), 0, SLABS)
    return values.at[chosen_slab].set(PROMPT_DEV).astype(jnp.int32)


def touch_ends(values, key, low, top_value):
    index_at = [jax.random.randint(jax.random.fold_in(key, axis), (), 0, length) for axis, length in enumerate(values.shape)]
    longest = values.shape.index(max(values.shape))
    beside = index_at[:longest] + [(index_at[longest] + 1) % values.shape[longest]] + index_at[longest + 1:]
    return values.at[tuple(index_at)].set(low).at[tuple(beside)].set(top_value)


def level_of(key, dims, cuts, least, top_value):
    level = 1.0
    for position, shards_of in cuts:
        heights = jax.random.uniform(jax.random.fold_in(jax.random.fold_in(key, 6), position), (shards_of,), jnp.float32, least / len(cuts), top_value / len(cuts))
        level = level * jnp.repeat(jnp.exp(heights), dims[position] // shards_of).reshape((-1,) + (1,) * (len(dims) - 1 - position))
    return level


def scatter_about(rng, dims, width, limit, split=(), kind=jnp.bfloat16):
    array = width * jax.random.normal(rng, dims, jnp.float32)
    if split:
        array = array * level_of(rng, dims, split, -0.22, 0.18)
    return jnp.clip(array, -limit, limit).astype(kind)


def setup_inputs(seed: int = 0) -> dict:
    arg_keys = jax.random.split(jax.random.key(seed), 5)
    return {
        "activations": scatter_about(arg_keys[0], (ROWS, D), 1.0, 6.0, ((0, 128), (1, 4))),
        "cand_index": touch_ends(jax.random.randint(arg_keys[1], (ROWS,), 0, CANDS), jax.random.fold_in(arg_keys[1], 1), 0, CANDS - 1).astype(jnp.int32),
        "labels": touch_ends((jax.random.randint(arg_keys[2], (PROMPTS,), 0, 2) < 1).astype(jnp.int32), jax.random.fold_in(arg_keys[2], 1), 0, 1),
        "counts": draw_counts(jax.random.fold_in(arg_keys[4], 71), 0),
    }


epsilon = 1e-06

def reference(activations, cand_index, labels, counts):
    row_total = activations.shape[0]
    row_ids = jnp.arange(row_total, dtype=jnp.int32)
    slab_of = row_ids // ROW_DEV
    prompt_of = row_ids // PER_PROMPT
    live = prompt_of % PROMPT_DEV < counts[slab_of]
    classes = labels[prompt_of]
    cand_ids = jnp.arange(CANDS, dtype=jnp.int32)
    matches = (cand_index[None, :] == cand_ids[:, None]) & live[None, :]
    harmful_hits = matches & (classes[None, :] == 1)
    harmless_hits = matches & (classes[None, :] == 0)
    member = jnp.concatenate([harmful_hits, harmless_hits], axis=0).astype(jnp.bfloat16)
    class_sums = jnp.dot(member, activations, preferred_element_type=jnp.float32)
    class_counts = lax.optimization_barrier(jnp.sum(member.astype(jnp.float32), axis=1))
    harmful_mean = class_sums[:CANDS] / jnp.maximum(class_counts[:CANDS], 1.0)[:, None]
    harmless_mean = class_sums[CANDS:] / jnp.maximum(class_counts[CANDS:], 1.0)[:, None]
    raw_dir = (harmful_mean - harmless_mean).astype(jnp.bfloat16)
    squares = lax.optimization_barrier(jnp.sum(jnp.square(raw_dir.astype(jnp.float32)), axis=1))
    inv_norm = lax.rsqrt(squares + epsilon).astype(jnp.bfloat16)
    plain = jnp.dot(activations, raw_dir.T, preferred_element_type=jnp.float32)
    return plain * inv_norm.astype(jnp.float32)[None, :]
```

```python
import functools

import jax
import jax.numpy as jnp
from jax import lax
from jax.experimental import pallas as pl
from jax.experimental.pallas import tpu as pltpu
from jax.sharding import PartitionSpec as P

CANDS = 128
PER_PROMPT = 16
EPSILON = 1e-06
MESH = pl.DeviceIdType.MESH
NT = (((1,), (1,)), ((), ()))


def order_of(n):
    return sorted(range(1, n), key=lambda k: -min(k, n - k))


def kernel(
    n, nx, act_ref, cand_ref, label_ref, live_ref, out_ref,
    act, member, xsend, xrecv, mine, part, ring, part2, ring2, unit, dirs, flat,
    proj, prec, cnt, cntr, sq, sqr,
    act_sem, cs, cr, xs, xr, s1, r1, s2, r2, g2s, g2r, g1s, g1r, gcs, gcr,
    ps, pr, qs, qr,
):
    rows, width = act_ref.shape
    half = width // 2
    cols = half // 2
    cu, fu = CANDS // n, half // n
    xb = CANDS // nx

    dp = lax.axis_index("dp")
    x = lax.axis_index("feat")
    c = lax.rem(dp, 2)
    z = lax.rem(dp // 2, n)
    y = dp // (2 * n)

    def at(yy, zz, cc, xx):
        return ((yy * n + zz) * 2 + cc, xx)

    other = 1 - c

    def along(axis, k):
        if axis == "y":
            return at(lax.rem(y + k, n), z, c, x)
        if axis == "z":
            return at(y, lax.rem(z + k, n), c, x)
        if axis == "x":
            return at(y, z, c, lax.rem(x + k, nx))
        if axis == "a":
            return at(
                lax.rem(y + other * k, n), lax.rem(z + c * k, n), c, x
            )
        return at(lax.rem(y + c * k, n), lax.rem(z + other * k, n), c, x)

    a = other * y + c * z
    b = other * z + c * y
    peer = at(y, z, other, x)

    def remote(src, dst, ss, rs, to):
        return pltpu.make_async_remote_copy(
            src_ref=src, dst_ref=dst, send_sem=ss, recv_sem=rs,
            device_id=to, device_id_type=MESH,
        )

    barrier = pltpu.get_barrier_semaphore()
    pl.semaphore_signal(barrier, inc=1, device_id=peer, device_id_type=MESH)
    for axis, size in (("y", n), ("z", n), ("x", nx)):
        for k in range(1, size):
            pl.semaphore_signal(
                barrier, inc=1, device_id=along(axis, k), device_id_type=MESH
            )

    loads = []
    for t in range(4):
        q = lax.rem(other * 2 + t, 4)
        load = pltpu.make_async_copy(
            act_ref.at[:, pl.ds(pl.multiple_of(q * cols, cols), cols)],
            act.at[q], act_sem.at[t],
        )
        load.start()
        loads.append((q, load))

    prompts = label_ref.shape[1]
    lab = label_ref[...]
    slot = lax.broadcasted_iota(jnp.int32, (8, prompts), 1)
    kind = lax.broadcasted_iota(jnp.int32, (8, prompts), 0)
    wanted = (lab == 1 - kind) & (kind < 2) & (slot < live_ref[...])
    by_prompt = jnp.where(wanted, 1.0, 0.0).astype(jnp.bfloat16)
    spread = jnp.where(
        lax.broadcasted_iota(jnp.int32, (prompts, rows), 1) // PER_PROMPT
        == lax.broadcasted_iota(jnp.int32, (prompts, rows), 0), 1.0, 0.0,
    ).astype(jnp.bfloat16)
    by_row = jnp.dot(by_prompt, spread, preferred_element_type=jnp.float32)
    hit = jnp.where(
        cand_ref[...] == lax.broadcasted_iota(jnp.int32, (CANDS, rows), 0), 1.0, 0.0
    )
    cnt[0] = lax.dot_general(
        by_row.astype(jnp.bfloat16), hit.astype(jnp.bfloat16), NT,
        preferred_element_type=jnp.float32,
    )
    member[0:CANDS, :] = (hit * by_row[0:1, :]).astype(jnp.bfloat16)
    member[CANDS:, :] = (hit * by_row[1:2, :]).astype(jnp.bfloat16)

    pl.semaphore_wait(barrier, 1 + 2 * (n - 1) + nx - 1)

    pending = []
    copy = remote(cnt.at[0], cntr.at[0], cs.at[0], cr.at[0], peer)
    copy.start()
    pending.append(copy)

    pair = []
    for t in range(2):
        q, load = loads[t]
        load.wait()
        xsend[t] = jnp.dot(
            member[...], act[q], preferred_element_type=jnp.float32
        )
        copy = remote(xsend.at[t], xrecv.at[t], xs.at[t], xr.at[t], peer)
        copy.start()
        pair.append(copy)
        if t == 0:
            pending[0].wait_recv()
            cnt[1] = cnt[0] + cntr[0]
            for k in order_of(n):
                copy = remote(
                    cnt.at[1], cntr.at[k], cs.at[k], cr.at[k], along("y", k)
                )
                copy.start()
                pending.append(copy)

    for t in range(2):
        q, load = loads[2 + t]
        load.wait()
        mine[t] = jnp.dot(
            member[...], act[q], preferred_element_type=jnp.float32
        )
        if t == 0:
            total = cnt[1]
            for copy in pending[1:]:
                copy.wait_recv()
            for k in range(1, n):
                total = total + cntr[k]
            cnt[2] = total
            for k in order_of(n):
                copy = remote(
                    cnt.at[2], cntr.at[n - 1 + k], cs.at[n - 1 + k],
                    cr.at[n - 1 + k], along("z", k),
                )
                copy.start()
                pending.append(copy)

    for copy in pending[n:]:
        copy.wait_recv()
    total = cnt[2]
    for k in range(n, 2 * n - 1):
        total = total + cntr[k]
    scale = 1.0 / jnp.maximum(total, 1.0)
    eye = (
        lax.broadcasted_iota(jnp.int32, (CANDS, CANDS), 0)
        == lax.broadcasted_iota(jnp.int32, (CANDS, CANDS), 1)
    )
    harmful = jnp.sum(jnp.where(eye, scale[0:1, :], 0.0), axis=1, keepdims=True)
    harmless = jnp.sum(jnp.where(eye, scale[1:2, :], 0.0), axis=1, keepdims=True)

    for t in range(2):
        pair[t].wait_recv()
        diff = (
            (mine[t, 0:CANDS, :] + xrecv[t, 0:CANDS, :]) * harmful
            - (mine[t, CANDS:, :] + xrecv[t, CANDS:, :]) * harmless
        )
        for i in range(n):
            for jj in range(n // 2):
                j = t * (n // 2) + jj
                u = other * (i * n + j) + c * (j * n + i)
                part[u] = diff[i * cu:(i + 1) * cu, jj * fu:(jj + 1) * fu]

    first = []
    for k in order_of(n):
        to = lax.rem(a + k, n)
        copy = remote(
            part.at[pl.ds(to * n, n)], ring.at[k], s1.at[k], r1.at[k], along("a", k)
        )
        copy.start()
        first.append(copy)
    for copy in first:
        copy.wait_recv()
    for u in range(n):
        total = part[a * n + u]
        for k in range(1, n):
            total = total + ring[k, u]
        part2[u] = total

    second = []
    for k in order_of(n):
        to = lax.rem(b + k, n)
        copy = remote(part2.at[to], ring2.at[k], s2.at[k], r2.at[k], along("b", k))
        copy.start()
        second.append(copy)
    for copy in second:
        copy.wait_recv()
    total = part2[b]
    for k in range(1, n):
        total = total + ring2[k]
    dirs[c, a * n + b] = total.astype(jnp.bfloat16)

    third = []
    for k in order_of(n):
        here = dirs.at[c, a * n + b]
        copy = remote(here, here, g2s.at[k], g2r.at[k], along("b", k))
        copy.start()
        third.append(copy)
    for copy in third:
        copy.wait_recv()
    fourth = []
    here = dirs.at[c, pl.ds(a * n, n)]
    for k in order_of(n):
        copy = remote(here, here, g1s.at[k], g1r.at[k], along("a", k))
        copy.start()
        fourth.append(copy)
    for copy in fourth:
        copy.wait_recv()
    across = remote(dirs.at[c], dirs.at[c], gcs.at[0], gcr.at[0], peer)
    across.start()
    across.wait_recv()

    squares = jnp.zeros((CANDS, 1), jnp.float32)
    for h in range(2):
        for i in range(n):
            for j in range(n):
                u = i * n + j if h == 0 else j * n + i
                flat[i * cu:(i + 1) * cu, h * half + j * fu:h * half + (j + 1) * fu] = (
                    dirs[h, u]
                )
    full = flat[...].astype(jnp.float32)
    squares = jnp.sum(full * full, axis=1, keepdims=True)
    sq[...] = jnp.broadcast_to(
        jnp.sum(jnp.where(eye, squares, 0.0), axis=0, keepdims=True), (8, CANDS)
    )
    squared = []
    for k in order_of(nx):
        copy = remote(sq, sqr.at[k], qs.at[k], qr.at[k], along("x", k))
        copy.start()
        squared.append(copy)

    parts = proj.shape[0]
    span = rows // parts
    sent = []
    for t in range(parts):
        total = jnp.zeros((CANDS, span), jnp.float32)
        for q in range(4):
            total = total + lax.dot_general(
                flat[:, q * cols:(q + 1) * cols],
                act[q, t * span:(t + 1) * span, :], NT,
                preferred_element_type=jnp.float32,
            )
        for k in range(nx):
            proj[t, k] = total[k * xb:(k + 1) * xb, :]
        for k in order_of(nx):
            to = lax.rem(x + k, nx)
            copy = remote(
                proj.at[t, to], prec.at[t, k], ps.at[t, k], pr.at[t, k],
                along("x", k),
            )
            copy.start()
            sent.append(copy)

    for copy in squared:
        copy.wait_recv()
    total = sq[...]
    for k in range(1, nx):
        total = total + sqr[k]
    inv = lax.rsqrt(total[0:1, :] + EPSILON).astype(jnp.bfloat16).astype(jnp.float32)
    own = (
        lax.broadcasted_iota(jnp.int32, (xb, CANDS), 0) + x * xb
        == lax.broadcasted_iota(jnp.int32, (xb, CANDS), 1)
    )
    inv = jnp.sum(jnp.where(own, inv, 0.0), axis=1, keepdims=True)
    for t in range(parts):
        for copy in sent[t * (nx - 1):(t + 1) * (nx - 1)]:
            copy.wait_recv()
        total = proj[t, x]
        for k in range(1, nx):
            total = total + prec[t, k]
        out_ref[:, t * span:(t + 1) * span] = total * inv

    for copy in [
        *pending, *pair, *first, *second, *third, *fourth, across, *squared, *sent
    ]:
        copy.wait_send()


def per_device(n, nx, activations, cand_index, labels, counts):
    rows, width = activations.shape
    half = width // 2
    cols = half // 2
    cu, fu = CANDS // n, half // n
    xb = CANDS // nx
    parts = 2
    f32, bf16, dma = jnp.float32, jnp.bfloat16, pltpu.SemaphoreType.DMA
    vmem = pl.BlockSpec(memory_space=pltpu.VMEM)
    out = pl.pallas_call(
        functools.partial(kernel, n, nx),
        out_shape=jax.ShapeDtypeStruct((xb, rows), f32),
        in_specs=[pl.BlockSpec(memory_space=pltpu.HBM), vmem, vmem, vmem],
        out_specs=vmem,
        scratch_shapes=[
            pltpu.VMEM((4, rows, cols), bf16),
            pltpu.VMEM((2 * CANDS, rows), bf16),
            pltpu.VMEM((2, 2 * CANDS, cols), f32),
            pltpu.VMEM((2, 2 * CANDS, cols), f32),
            pltpu.VMEM((2, 2 * CANDS, cols), f32),
            pltpu.VMEM((n * n, cu, fu), f32),
            pltpu.VMEM((n, n, cu, fu), f32),
            pltpu.VMEM((n, cu, fu), f32),
            pltpu.VMEM((n, cu, fu), f32),
            pltpu.VMEM((cu, fu), f32),
            pltpu.VMEM((2, n * n, cu, fu), bf16),
            pltpu.VMEM((CANDS, width), bf16),
            pltpu.VMEM((parts, nx, xb, rows // parts), f32),
            pltpu.VMEM((parts, nx, xb, rows // parts), f32),
            pltpu.VMEM((3, 8, CANDS), f32),
            pltpu.VMEM((2 * n - 1, 8, CANDS), f32),
            pltpu.VMEM((8, CANDS), f32),
            pltpu.VMEM((nx, 8, CANDS), f32),
            dma((4,)), dma((2 * n - 1,)), dma((2 * n - 1,)), dma((2,)), dma((2,)),
            dma((n,)), dma((n,)), dma((n,)), dma((n,)),
            dma((n,)), dma((n,)), dma((n,)), dma((n,)), dma((1,)), dma((1,)),
            dma((parts, nx)), dma((parts, nx)), dma((nx,)), dma((nx,)),
        ],
        compiler_params=pltpu.CompilerParams(
            collective_id=0, has_side_effects=True, vmem_limit_bytes=48 << 20
        ),
        name="directions",
    )(
        activations,
        cand_index.reshape(1, rows),
        labels.reshape(1, -1),
        counts.reshape(1, 1),
    )
    return out.T


def solution(mesh):
    n = 1
    while 2 * n * n < mesh.shape["dp"]:
        n *= 2
    return jax.shard_map(
        functools.partial(per_device, n, mesh.shape["feat"]),
        mesh=mesh,
        in_specs=(P("dp", "feat"), P("dp"), P("dp"), P("dp")),
        out_specs=P("dp", "feat"),
        check_vma=False,
    )
```
